32 devices in a mesh: ha: 8 (over y, x, core), col: 4 (over z).
Axes of the slice: x: 2, y: 2, z: 4, core: 2. Of those that a mesh axis runs over, the one named last changes fastest.
Arguments:
- features: bfloat16 [3, 32, 128, 512], P(None, 'ha', 'col'), may hold values from -18 to 18
Outputs:
- lag_cov: float32 [128, 16000], P('col', 'ha')
The draws below stay inside these ranges and needn't reach their ends.
All inputs are finite; a program needn't handle non-finite values.
Results may differ from the reference program's by a relative error of at most 0.0003.
Values may be sent and summed in bfloat16 or wider, within the bound.
A program may use at most 384 MiB of HBM per device.

```python
import jax
import jax.numpy as jnp
from jax import lax

C = 128
W = 512
TF = 3
H = 32


def draw_features(key, part):
    keys = jax.random.split(key, 9)
    rough_field = jnp.clip(jax.random.normal(keys[0], (TF, H, C, W), jnp.float32), -5.0, 5.0)
    weight_scale = 0.6
    mix_spread = 0.5
    loads = jnp.clip(jax.random.normal(keys[1], (6, C), jnp.float32) * weight_scale, -1.5, 1.5)
    wave_w = jax.random.uniform(keys[2], (6,), jnp.float32, 0.05, 0.9)
    wave_h = jax.random.uniform(keys[3], (6,), jnp.float32, 0.05, 0.9)
    wave_t = jax.random.uniform(keys[4], (6,), jnp.float32, 0.2, 1.5)
    phases = jax.random.uniform(keys[5], (6,), jnp.float32, 0.0, 6.2831853)
    frame_pos = jnp.arange(TF, dtype=jnp.float32)[:, None, None, None]
    row_pos = jnp.arange(H, dtype=jnp.float32)[None, :, None, None]
    column_pos = jnp.arange(W, dtype=jnp.float32)[None, None, None, :]
    kernels = jax.random.normal(keys[6], (27, C), jnp.float32) * 0.19245
    padded_rough = jnp.pad(rough_field, ((1, 1), (1, 1), (0, 0), (1, 1)))
    smooth_field = jnp.zeros((TF, H, C, W), jnp.float32)
    tap_index = 0
    for step_t in range(3):
        for step_h in range(3):
            for step_w in range(3):
                smooth_field = smooth_field + kernels[tap_index][None, None, :, None] * padded_rough[step_t:step_t + TF, step_h:step_h + H, :, step_w:step_w + W]
                tap_index = tap_index + 1
    groups = C // 8
    inner_mix = jnp.eye(8, dtype=jnp.float32)[None, :, :] + mix_spread * 0.35355 * jax.random.normal(keys[7], (groups, 8, 8), jnp.float32)
    outer_mix = jnp.eye(groups, dtype=jnp.float32)[None, :, :] + mix_spread * groups ** (-0.5) * jax.random.normal(keys[8], (8, groups, groups), jnp.float32)
    grouped = smooth_field.reshape(TF, H, groups, 8, W)
    section_mix = jnp.zeros((TF, H, groups, 8, W), jnp.float32)
    for source in range(8):
        section_mix = section_mix + inner_mix[:, :, source][None, None, :, :, None] * grouped[:, :, :, source:source + 1, :]
    mixed_field = jnp.zeros((TF, H, groups, 8, W), jnp.float32)
    for source in range(groups):
        outer_column = jnp.transpose(outer_mix[:, :, source], (1, 0))
        mixed_field = mixed_field + outer_column[None, None, :, :, None] * section_mix[:, :, source:source + 1, :, :]
    result = 1.5 * mixed_field.reshape(TF, H, C, W)
    for component in range(6):
        angle_field = wave_w[component] * column_pos + wave_h[component] * row_pos + wave_t[component] * frame_pos + phases[component]
        result = result + 1.4142 * loads[component][None, None, :, None] * jnp.cos(angle_field)
    return jnp.clip(result, -18.0, 18.0).astype(jnp.bfloat16)


def setup_inputs(seed: int = 0) -> dict:
    key_list = jax.random.split(jax.random.key(seed), 2)
    features = draw_features(jax.random.fold_in(key_list[1], 71), 0)
    return dict(features=features)


def reference(features):
    fields = jnp.transpose(features.astype(jnp.float32), (2, 0, 1, 3))
    own_rows = fields.reshape(C, -1)
    padded = jnp.pad(fields, ((0, 0), (2, 2), (2, 2), (2, 2)))
    position_count = TF * H * W

    def lag_cov(lag_index):
        step_t = lag_index // 25
        step_h = (lag_index // 5) % 5
        step_w = lag_index % 5
        zero_index = jnp.zeros((), jnp.int32)
        shifted = lax.dynamic_slice(padded, (zero_index, step_t.astype(jnp.int32), step_h.astype(jnp.int32), step_w.astype(jnp.int32)), (C, TF, H, W))
        other_rows = shifted.reshape(C, -1)
        return jnp.dot(own_rows, other_rows.T, precision=lax.Precision.HIGHEST, preferred_element_type=jnp.float32) / position_count

    blocks = lax.map(lag_cov, jnp.arange(125, dtype=jnp.int32))
    return jnp.transpose(blocks, (1, 0, 2)).reshape(C, 125 * C)
```

```python
import functools

import jax
import jax.numpy as jnp
from jax import lax
from jax.experimental import pallas as pl
from jax.experimental.pallas import tpu as pltpu
from jax.sharding import PartitionSpec as P

MESH = pl.DeviceIdType.MESH
REACH = 2
STEPS = 2 * REACH + 1


def window_plan(lag_count, channels, ha_count):
    share = lag_count * channels // ha_count
    spans = [-(-(i + 1) * share // channels) - i * share // channels for i in range(ha_count)]
    return share, max(spans)


def kernel(
    ha_count, col_count, x_ref, out_ref, base, stack, others, part, near, mixed, far,
    local_sem, halo_send, halo_recv, line_send, line_recv, near_send, near_recv, far_send, far_recv,
):
    frames, rows, block, width = x_ref.shape
    channels = block * col_count
    lag_count = STEPS**3
    share, span = window_plan(lag_count, channels, ha_count)
    i, j = lax.axis_index("ha"), lax.axis_index("col")
    half = ha_count // 2
    parity, place = lax.rem(i, 2), lax.div(i, 2)
    partner = i + 1 - 2 * parity

    def first_lag(index):
        return jnp.minimum(lax.div(index * share, channels), lag_count - span)

    barrier = pltpu.get_barrier_semaphore()
    for step in range(1, ha_count):
        pl.semaphore_signal(
            barrier, inc=1, device_id={"ha": lax.rem(i + step, ha_count)}, device_id_type=MESH
        )

    @pl.when(j > 0)
    def _():
        pl.semaphore_signal(barrier, inc=1, device_id={"col": j - 1}, device_id_type=MESH)

    @pl.when(j < col_count - 1)
    def _():
        pl.semaphore_signal(barrier, inc=1, device_id={"col": j + 1}, device_id_type=MESH)

    own_copies = []
    for h in range(rows):
        own_copies.append(
            pltpu.make_async_copy(
                x_ref.at[:, h], others.at[:, j, :, pl.ds(h * width, width)], local_sem.at[0, h]
            )
        )
        own_copies.append(
            pltpu.make_async_copy(
                x_ref.at[:, h], base.at[:, :, pl.ds((h + REACH) * width, width)], local_sem.at[1, h]
            )
        )
    for copy in own_copies:
        copy.start()

    ends = (j > 0).astype(jnp.int32) + (j < col_count - 1).astype(jnp.int32)
    pl.semaphore_wait(barrier, ha_count - 1 + ends)

    def halo(way, r):
        source = rows - REACH + r if way == 0 else r
        slot = r if way == 0 else rows + REACH + r
        return pltpu.make_async_remote_copy(
            src_ref=x_ref.at[:, source],
            dst_ref=base.at[:, :, pl.ds(slot * width, width)],
            send_sem=halo_send.at[way, r],
            recv_sem=halo_recv.at[way, r],
            device_id={"ha": (i + 1) if way == 0 else (i - 1)},
            device_id_type=MESH,
        )

    has_after, has_before = i < ha_count - 1, i > 0
    for way, has in ((0, has_after), (1, has_before)):

        @pl.when(has)
        def _():
            for r in range(REACH):
                halo(way, r).start()

    for copy in own_copies:
        copy.wait()

    def hop(way, step):
        sign = 1 if way == 0 else -1
        owner = j - sign * step
        return pltpu.make_async_remote_copy(
            src_ref=others.at[:, owner],
            dst_ref=others.at[:, owner],
            send_sem=line_send.at[way, step],
            recv_sem=line_recv.at[way, step],
            device_id={"col": j + sign},
            device_id_type=MESH,
        )

    def sends(way, step):
        if way == 0:
            return jnp.logical_and(j < col_count - 1, j - step >= 0)
        return jnp.logical_and(j > 0, j + step <= col_count - 1)

    def receives(way, step):
        return j - 1 - step >= 0 if way == 0 else j + 1 + step <= col_count - 1

    def arrival(way, step):
        sign = 1 if way == 0 else -1
        owner = j - sign * (step + 1)
        return pltpu.make_async_remote_copy(
            src_ref=others.at[:, owner],
            dst_ref=others.at[:, owner],
            send_sem=line_send.at[way, step],
            recv_sem=line_recv.at[way, step],
            device_id={"col": j - sign},
            device_id_type=MESH,
        )

    for way in range(2):

        @pl.when(sends(way, 0))
        def _():
            hop(way, 0).start()

    @pl.when(jnp.logical_not(has_before))
    def _():
        base[:, :, : REACH * width] = jnp.zeros((frames, block, REACH * width), base.dtype)

    @pl.when(jnp.logical_not(has_after))
    def _():
        base[:, :, (rows + REACH) * width :] = jnp.zeros((frames, block, REACH * width), base.dtype)

    for way, has_in in ((0, has_before), (1, has_after)):

        @pl.when(has_in)
        def _():
            for r in range(REACH):
                halo(way, r).wait_recv()

    column = lax.broadcasted_iota(jnp.int32, (block, width), 1)

    def shift_row(index, carry):
        t, h = lax.div(index, rows + 2 * REACH), lax.rem(index, rows + 2 * REACH)
        lanes = pl.ds(pl.multiple_of(h * width, width), width)
        plain = base[t, :, lanes]
        wide = plain.astype(jnp.float32)
        for step_w in range(STEPS):
            shift = step_w - REACH
            if shift == 0:
                stack[step_w, t, :, lanes] = plain
            else:
                moved = pltpu.roll(wide, shift % width, axis=1)
                keep = column >= shift if shift > 0 else column < width + shift
                stack[step_w, t, :, lanes] = jnp.where(keep, moved, 0.0).astype(plain.dtype)
        return carry

    lax.fori_loop(0, frames * (rows + 2 * REACH), shift_row, 0)

    for step in range(col_count - 1):
        for way in range(2):

            @pl.when(receives(way, step))
            def _():
                arrival(way, step).wait_recv()

            if step + 1 < col_count - 1:

                @pl.when(sends(way, step + 1))
                def _():
                    hop(way, step + 1).start()

    depth = rows * width
    scale = 1.0 / (frames * rows * ha_count * width)

    def products(step_h, carry):
        start = pl.multiple_of((STEPS - 1 - step_h) * width, width)
        own = stack[:, :, :, pl.ds(start, depth)].reshape(STEPS * frames * block, depth)
        field = others[...].reshape(frames * channels, depth)
        result = lax.dot_general(
            own, field, (((1,), (1,)), ((), ())), preferred_element_type=jnp.float32
        ).reshape(STEPS, frames, block, frames * channels)
        for step_w in range(STEPS):
            for step_t in range(STEPS):
                shift = step_t - REACH
                total = None
                for t in range(frames):
                    if 0 <= t + shift < frames:
                        term = result[step_w, t, :, (t + shift) * channels : (t + shift + 1) * channels]
                        total = term if total is None else total + term
                if total is None:
                    total = jnp.zeros((block, channels), jnp.float32)
                part[step_t * STEPS * STEPS + step_h * STEPS + step_w] = total * scale
        return carry

    lax.fori_loop(0, STEPS, products, 0)

    near_copies = []
    for m in range(half):
        near_copies.append(
            pltpu.make_async_remote_copy(
                src_ref=part.at[pl.ds(first_lag(2 * m + 1 - parity), span)],
                dst_ref=near.at[m],
                send_sem=near_send.at[m],
                recv_sem=near_recv.at[m],
                device_id={"ha": partner},
                device_id_type=MESH,
            )
        )
    for copy in near_copies:
        copy.start()
    far_copies = {}
    for m in range(half):
        near_copies[m].wait_recv()
        mixed[m] = part[pl.ds(first_lag(2 * m + parity), span)] + near[m]
    for r in range(1, half):
        target = lax.rem(place + r, half)
        far_copies[r] = pltpu.make_async_remote_copy(
            src_ref=mixed.at[target],
            dst_ref=far.at[r - 1],
            send_sem=far_send.at[r - 1],
            recv_sem=far_recv.at[r - 1],
            device_id={"ha": 2 * target + parity},
            device_id_type=MESH,
        )
        far_copies[r].start()
    for r in range(1, half):
        far_copies[r].wait_recv()
    for k in range(span):
        total = mixed[place, k]
        for r in range(1, half):
            total = total + far[r - 1, k]
        out_ref[:, k * channels : (k + 1) * channels] = total

    for r in range(1, half):
        far_copies[r].wait_send()
    for copy in near_copies:
        copy.wait_send()
    for step in range(col_count - 1):
        for way in range(2):

            @pl.when(sends(way, step))
            def _():
                hop(way, step).wait_send()

    for way, has in ((0, has_after), (1, has_before)):

        @pl.when(has)
        def _():
            for r in range(REACH):
                halo(way, r).wait_send()


def body(ha_count, col_count, features):
    frames, rows, block, width = features.shape
    channels = block * col_count
    lag_count = STEPS**3
    share, span = window_plan(lag_count, channels, ha_count)
    half = ha_count // 2
    dma = pltpu.SemaphoreType.DMA
    lines = max(col_count - 1, 1)
    window = pl.pallas_call(
        functools.partial(kernel, ha_count, col_count),
        out_shape=jax.ShapeDtypeStruct((block, span * channels), jnp.float32),
        in_specs=[pl.BlockSpec(memory_space=pl.ANY)],
        out_specs=pl.BlockSpec(memory_space=pltpu.VMEM),
        scratch_shapes=[
            pltpu.VMEM((frames, block, (rows + 2 * REACH) * width), features.dtype),
            pltpu.VMEM((STEPS, frames, block, (rows + 2 * REACH) * width), features.dtype),
            pltpu.VMEM((frames, col_count, block, rows * width), features.dtype),
            pltpu.VMEM((lag_count, block, channels), jnp.float32),
            pltpu.VMEM((half, span, block, channels), jnp.float32),
            pltpu.VMEM((half, span, block, channels), jnp.float32),
            pltpu.VMEM((half, span, block, channels), jnp.float32),
            dma((2, rows)),
            dma((2, REACH)),
            dma((2, REACH)),
            dma((2, lines)),
            dma((2, lines)),
            dma((half,)),
            dma((half,)),
            dma((half,)),
            dma((half,)),
        ],
        compiler_params=pltpu.CompilerParams(collective_id=0, has_side_effects=True),
        name="lag_cov",
    )(features)
    i = lax.axis_index("ha")
    first = jnp.minimum(i * share // channels, lag_count - span)
    return lax.dynamic_slice_in_dim(window, i * share - first * channels, share, 1)


def solution(mesh):
    in_specs = (P(None, "ha", "col", None),)
    out_specs = P("col", "ha")
    counts = (mesh.shape["ha"], mesh.shape["col"])
    return jax.shard_map(
        functools.partial(body, *counts), mesh=mesh, in_specs=in_specs, out_specs=out_specs, check_vma=False
    )
```

```python
import functools

import jax
import jax.numpy as jnp
from jax import lax
from jax.experimental import pallas as pl
from jax.experimental.pallas import tpu as pltpu
from jax.sharding import PartitionSpec as P

MESH = pl.DeviceIdType.MESH
REACH = 2
STEPS = 2 * REACH + 1


def window_plan(lag_count, channels, ha_count):
    share = lag_count * channels // ha_count
    spans = [-(-(i + 1) * share // channels) - i * share // channels for i in range(ha_count)]
    return share, max(spans)


def kernel(
    ha_count, col_count, x_ref, out_ref, base, stack, others, part, near, mixed, far, summed,
    local_sem, halo_send, halo_recv, line_send, line_recv, near_send, near_recv, far_send, far_recv,
):
    frames, rows, block, width = x_ref.shape
    channels = block * col_count
    lag_count = STEPS**3
    share, span = window_plan(lag_count, channels, ha_count)
    i, j = lax.axis_index("ha"), lax.axis_index("col")
    half = ha_count // 2
    parity, place = lax.rem(i, 2), lax.div(i, 2)
    partner = i + 1 - 2 * parity

    def first_lag(index):
        return jnp.minimum(lax.div(index * share, channels), lag_count - span)

    barrier = pltpu.get_barrier_semaphore()
    for step in range(1, ha_count):
        pl.semaphore_signal(
            barrier, inc=1, device_id={"ha": lax.rem(i + step, ha_count)}, device_id_type=MESH
        )

    @pl.when(j > 0)
    def _():
        pl.semaphore_signal(barrier, inc=1, device_id={"col": j - 1}, device_id_type=MESH)

    @pl.when(j < col_count - 1)
    def _():
        pl.semaphore_signal(barrier, inc=1, device_id={"col": j + 1}, device_id_type=MESH)

    own_copies = []
    for h in range(rows):
        own_copies.append(
            pltpu.make_async_copy(
                x_ref.at[:, h], others.at[:, j, :, pl.ds(h * width, width)], local_sem.at[0, h]
            )
        )
        own_copies.append(
            pltpu.make_async_copy(
                x_ref.at[:, h], base.at[:, :, pl.ds((h + REACH) * width, width)], local_sem.at[1, h]
            )
        )
    for copy in own_copies:
        copy.start()

    ends = (j > 0).astype(jnp.int32) + (j < col_count - 1).astype(jnp.int32)
    pl.semaphore_wait(barrier, ha_count - 1 + ends)

    def halo(way, r):
        source = rows - REACH + r if way == 0 else r
        slot = r if way == 0 else rows + REACH + r
        return pltpu.make_async_remote_copy(
            src_ref=x_ref.at[:, source],
            dst_ref=base.at[:, :, pl.ds(slot * width, width)],
            send_sem=halo_send.at[way, r],
            recv_sem=halo_recv.at[way, r],
            device_id={"ha": (i + 1) if way == 0 else (i - 1)},
            device_id_type=MESH,
        )

    has_after, has_before = i < ha_count - 1, i > 0
    for way, has in ((0, has_after), (1, has_before)):

        @pl.when(has)
        def _():
            for r in range(REACH):
                halo(way, r).start()

    for copy in own_copies:
        copy.wait()

    def hop(way, step, t):
        sign = 1 if way == 0 else -1
        owner = j - sign * step
        return pltpu.make_async_remote_copy(
            src_ref=others.at[t, owner],
            dst_ref=others.at[t, owner],
            send_sem=line_send.at[way, step, t],
            recv_sem=line_recv.at[way, step, t],
            device_id={"col": j + sign},
            device_id_type=MESH,
        )

    def sends(way, step):
        if way == 0:
            return jnp.logical_and(j < col_count - 1, j - step >= 0)
        return jnp.logical_and(j > 0, j + step <= col_count - 1)

    def receives(way, step):
        return j - 1 - step >= 0 if way == 0 else j + 1 + step <= col_count - 1

    def arrival(way, step, t):
        sign = 1 if way == 0 else -1
        owner = j - sign * (step + 1)
        return pltpu.make_async_remote_copy(
            src_ref=others.at[t, owner],
            dst_ref=others.at[t, owner],
            send_sem=line_send.at[way, step, t],
            recv_sem=line_recv.at[way, step, t],
            device_id={"col": j - sign},
            device_id_type=MESH,
        )

    for way in range(2):

        @pl.when(sends(way, 0))
        def _():
            for t in range(frames):
                hop(way, 0, t).start()

    @pl.when(jnp.logical_not(has_before))
    def _():
        base[:, :, : REACH * width] = jnp.zeros((frames, block, REACH * width), base.dtype)

    @pl.when(jnp.logical_not(has_after))
    def _():
        base[:, :, (rows + REACH) * width :] = jnp.zeros((frames, block, REACH * width), base.dtype)

    for way, has_in in ((0, has_before), (1, has_after)):

        @pl.when(has_in)
        def _():
            for r in range(REACH):
                halo(way, r).wait_recv()

    column = lax.broadcasted_iota(jnp.int32, (block, width), 1)

    def shift_row(index, carry):
        t, h = lax.div(index, rows + 2 * REACH), lax.rem(index, rows + 2 * REACH)
        lanes = pl.ds(pl.multiple_of(h * width, width), width)
        plain = base[t, :, lanes]
        wide = plain.astype(jnp.float32)
        for step_w in range(STEPS):
            shift = step_w - REACH
            if shift == 0:
                stack[step_w, t, :, lanes] = plain
            else:
                moved = pltpu.roll(wide, shift % width, axis=1)
                keep = column >= shift if shift > 0 else column < width + shift
                stack[step_w, t, :, lanes] = jnp.where(keep, moved, 0.0).astype(plain.dtype)
        return carry

    lax.fori_loop(0, frames * (rows + 2 * REACH), shift_row, 0)

    def advance(step):
        for t in range(frames):
            for way in range(2):

                @pl.when(receives(way, step))
                def _():
                    arrival(way, step, t).wait_recv()

                if step + 1 < col_count - 1:

                    @pl.when(sends(way, step + 1))
                    def _():
                        hop(way, step + 1, t).start()

    both = jnp.minimum(j, col_count - 1 - j)
    more_after = j < col_count - 1 - j

    def owner_of(slot):
        paired = j + ((slot + 1) // 2) * (1 if slot % 2 == 0 else -1)
        single = jnp.where(more_after, j + (slot - both), j - (slot - both))
        return jnp.where(slot <= 2 * both, paired, single)

    depth = rows * width
    group = block // col_count
    scale = 1.0 / (frames * rows * ha_count * width)
    lane_block = lax.broadcasted_iota(jnp.int32, (group, channels), 1) // block

    def compute(slot):
        owner = owner_of(slot)

        def products(step_h, carry):
            start = pl.multiple_of((STEPS - 1 - step_h) * width, width)
            own = stack[:, :, :, pl.ds(start, depth)].reshape(STEPS * frames * block, depth)
            field = others[:, owner].reshape(frames * block, depth)
            result = lax.dot_general(
                own, field, (((1,), (1,)), ((), ())), preferred_element_type=jnp.float32
            )
            spare = jnp.zeros((result.shape[0], channels - result.shape[1]), jnp.float32)
            result = jnp.concatenate([result * scale, spare], axis=1)
            moved = [result] + [pltpu.roll(result, k * block, axis=1) for k in range(1, col_count)]
            for step_w in range(STEPS):
                for step_t in range(STEPS):
                    shift = step_t - REACH
                    packed = jnp.zeros((group, channels), jnp.float32)
                    for g in range(col_count):
                        total = None
                        for t in range(frames):
                            if 0 <= t + shift < frames:
                                row = (step_w * frames + t) * block + g * group
                                term = moved[(g - t - shift) % col_count][row : row + group]
                                total = term if total is None else total + term
                        if total is not None:
                            packed = jnp.where(lane_block == g, total, packed)
                    part[slot, step_t * STEPS * STEPS + step_h * STEPS + step_w] = packed
            return carry

        lax.fori_loop(0, STEPS, products, 0)

    near_copies, far_copies = {}, {}

    def pass_near(slot):
        for m in range(half):
            near_copies[slot, m] = pltpu.make_async_remote_copy(
                src_ref=part.at[slot, pl.ds(first_lag(2 * m + 1 - parity), span)],
                dst_ref=near.at[slot, m],
                send_sem=near_send.at[slot, m],
                recv_sem=near_recv.at[slot, m],
                device_id={"ha": partner},
                device_id_type=MESH,
            )
            near_copies[slot, m].start()

    def pass_far(slot):
        for m in range(half):
            near_copies[slot, m].wait_recv()
            mixed[slot, m] = part[slot, pl.ds(first_lag(2 * m + parity), span)] + near[slot, m]
        for r in range(1, half):
            target = lax.rem(place + r, half)
            far_copies[slot, r] = pltpu.make_async_remote_copy(
                src_ref=mixed.at[slot, target],
                dst_ref=far.at[slot, r - 1],
                send_sem=far_send.at[slot, r - 1],
                recv_sem=far_recv.at[slot, r - 1],
                device_id={"ha": 2 * target + parity},
                device_id_type=MESH,
            )
            far_copies[slot, r].start()

    for slot in range(col_count):
        if slot > 0:
            advance(slot - 1)
            pass_far(slot - 1)
        compute(slot)
        pass_near(slot)
    pass_far(col_count - 1)

    for slot in range(col_count):
        for r in range(1, half):
            far_copies[slot, r].wait_recv()
        total = mixed[slot, place]
        for r in range(1, half):
            total = total + far[slot, r - 1]
        summed[owner_of(slot)] = total

    for k in range(span):
        tiles = [summed[q, k] for q in range(col_count)]
        for g in range(col_count):
            rows_out = jnp.zeros((group, channels), jnp.float32)
            for q in range(col_count):
                turn = (q - g) * block % channels
                tile = pltpu.roll(tiles[q], turn, axis=1) if turn else tiles[q]
                rows_out = jnp.where(lane_block == q, tile, rows_out)
            out_ref[g * group : (g + 1) * group, k * channels : (k + 1) * channels] = rows_out

    for copy in list(far_copies.values()) + list(near_copies.values()):
        copy.wait_send()
    for step in range(col_count - 1):
        for way in range(2):

            @pl.when(sends(way, step))
            def _():
                for t in range(frames):
                    hop(way, step, t).wait_send()

    for way, has in ((0, has_after), (1, has_before)):

        @pl.when(has)
        def _():
            for r in range(REACH):
                halo(way, r).wait_send()


def body(ha_count, col_count, features):
    frames, rows, block, width = features.shape
    channels = block * col_count
    lag_count = STEPS**3
    share, span = window_plan(lag_count, channels, ha_count)
    half = ha_count // 2
    group = block // col_count
    dma = pltpu.SemaphoreType.DMA
    lines = max(col_count - 1, 1)
    window = pl.pallas_call(
        functools.partial(kernel, ha_count, col_count),
        out_shape=jax.ShapeDtypeStruct((block, span * channels), jnp.float32),
        in_specs=[pl.BlockSpec(memory_space=pl.ANY)],
        out_specs=pl.BlockSpec(memory_space=pltpu.VMEM),
        scratch_shapes=[
            pltpu.VMEM((frames, block, (rows + 2 * REACH) * width), features.dtype),
            pltpu.VMEM((STEPS, frames, block, (rows + 2 * REACH) * width), features.dtype),
            pltpu.VMEM((frames, col_count, block, rows * width), features.dtype),
            pltpu.VMEM((col_count, lag_count, group, channels), jnp.float32),
            pltpu.VMEM((col_count, half, span, group, channels), jnp.float32),
            pltpu.VMEM((col_count, half, span, group, channels), jnp.float32),
            pltpu.VMEM((col_count, half, span, group, channels), jnp.float32),
            pltpu.VMEM((col_count, span, group, channels), jnp.float32),
            dma((2, rows)),
            dma((2, REACH)),
            dma((2, REACH)),
            dma((2, lines, frames)),
            dma((2, lines, frames)),
            dma((col_count, half)),
            dma((col_count, half)),
            dma((col_count, half)),
            dma((col_count, half)),
        ],
        compiler_params=pltpu.CompilerParams(collective_id=0, has_side_effects=True),
        name="lag_cov",
    )(features)
    i = lax.axis_index("ha")
    first = jnp.minimum(i * share // channels, lag_count - span)
    return lax.dynamic_slice_in_dim(window, i * share - first * channels, share, 1)


def solution(mesh):
    in_specs = (P(None, "ha", "col", None),)
    out_specs = P("col", "ha")
    counts = (mesh.shape["ha"], mesh.shape["col"])
    return jax.shard_map(
        functools.partial(body, *counts), mesh=mesh, in_specs=in_specs, out_specs=out_specs, check_vma=False
    )
```

```python
import functools

import jax
import jax.numpy as jnp
from jax import lax
from jax.experimental import pallas as pl
from jax.experimental.pallas import tpu as pltpu
from jax.sharding import PartitionSpec as P

MESH = pl.DeviceIdType.MESH
REACH = 2
STEPS = 2 * REACH + 1


def window_plan(lag_count, channels, ha_count):
    share = lag_count * channels // ha_count
    spans = [-(-(i + 1) * share // channels) - i * share // channels for i in range(ha_count)]
    return share, max(spans)


def kernel(
    ha_count, col_count, x_ref, out_ref, base, stack, others, part, near, mixed, far, summed, early,
    local_sem, halo_send, halo_recv, line_send, line_recv, near_send, near_recv, far_send, far_recv,
):
    frames, rows, block, width = x_ref.shape
    channels = block * col_count
    lag_count = STEPS**3
    share, span = window_plan(lag_count, channels, ha_count)
    i, j = lax.axis_index("ha"), lax.axis_index("col")
    half = ha_count // 2
    parity, place = lax.rem(i, 2), lax.div(i, 2)
    partner = i + 1 - 2 * parity

    def first_lag(index):
        return jnp.minimum(lax.div(index * share, channels), lag_count - span)

    barrier = pltpu.get_barrier_semaphore()
    for step in range(1, ha_count):
        pl.semaphore_signal(
            barrier, inc=1, device_id={"ha": lax.rem(i + step, ha_count)}, device_id_type=MESH
        )

    @pl.when(j > 0)
    def _():
        pl.semaphore_signal(barrier, inc=1, device_id={"col": j - 1}, device_id_type=MESH)

    @pl.when(j < col_count - 1)
    def _():
        pl.semaphore_signal(barrier, inc=1, device_id={"col": j + 1}, device_id_type=MESH)

    own_copies = []
    for h in range(rows):
        own_copies.append(
            pltpu.make_async_copy(
                x_ref.at[:, h], others.at[h, j], local_sem.at[0, h]
            )
        )
        own_copies.append(
            pltpu.make_async_copy(
                x_ref.at[:, h], base.at[:, :, pl.ds((h + REACH) * width, width)], local_sem.at[1, h]
            )
        )
    for copy in own_copies:
        copy.start()

    ends = (j > 0).astype(jnp.int32) + (j < col_count - 1).astype(jnp.int32)
    pl.semaphore_wait(barrier, ha_count - 1 + ends)

    def halo(way, r):
        source = rows - REACH + r if way == 0 else r
        slot = r if way == 0 else rows + REACH + r
        return pltpu.make_async_remote_copy(
            src_ref=x_ref.at[:, source],
            dst_ref=base.at[:, :, pl.ds(slot * width, width)],
            send_sem=halo_send.at[way, r],
            recv_sem=halo_recv.at[way, r],
            device_id={"ha": (i + 1) if way == 0 else (i - 1)},
            device_id_type=MESH,
        )

    def hop(way, step, h):
        sign = 1 if way == 0 else -1
        owner = j - sign * step
        return pltpu.make_async_remote_copy(
            src_ref=x_ref.at[:, h] if step == 0 else others.at[h, owner],
            dst_ref=others.at[h, owner],
            send_sem=line_send.at[way, step, h],
            recv_sem=line_recv.at[way, step, h],
            device_id={"col": j + sign},
            device_id_type=MESH,
        )

    def sends(way, step):
        if way == 0:
            return jnp.logical_and(j < col_count - 1, j - step >= 0)
        return jnp.logical_and(j > 0, j + step <= col_count - 1)

    def receives(way, step):
        return j - 1 - step >= 0 if way == 0 else j + 1 + step <= col_count - 1

    def arrival(way, step, h):
        sign = 1 if way == 0 else -1
        owner = j - sign * (step + 1)
        return pltpu.make_async_remote_copy(
            src_ref=others.at[h, owner],
            dst_ref=others.at[h, owner],
            send_sem=line_send.at[way, step, h],
            recv_sem=line_recv.at[way, step, h],
            device_id={"col": j - sign},
            device_id_type=MESH,
        )

    for way in range(2):

        @pl.when(sends(way, 0))
        def _():
            for h in range(rows):
                hop(way, 0, h).start()

    has_after, has_before = i < ha_count - 1, i > 0
    for way, has in ((0, has_after), (1, has_before)):

        @pl.when(has)
        def _():
            for r in range(REACH):
                halo(way, r).start()

    for copy in own_copies:
        copy.wait()

    @pl.when(jnp.logical_not(has_before))
    def _():
        base[:, :, : REACH * width] = jnp.zeros((frames, block, REACH * width), base.dtype)

    @pl.when(jnp.logical_not(has_after))
    def _():
        base[:, :, (rows + REACH) * width :] = jnp.zeros((frames, block, REACH * width), base.dtype)

    for way, has_in in ((0, has_before), (1, has_after)):

        @pl.when(has_in)
        def _():
            for r in range(REACH):
                halo(way, r).wait_recv()

    column = lax.broadcasted_iota(jnp.int32, (block, width), 1)

    def shift_row(index, carry):
        t, h = lax.div(index, rows + 2 * REACH), lax.rem(index, rows + 2 * REACH)
        lanes = pl.ds(pl.multiple_of(h * width, width), width)
        plain = base[t, :, lanes]
        wide = plain.astype(jnp.float32)
        for step_w in range(STEPS):
            shift = step_w - REACH
            if shift == 0:
                stack[step_w, t, :, lanes] = plain
            else:
                moved = pltpu.roll(wide, shift % width, axis=1)
                keep = column >= shift if shift > 0 else column < width + shift
                stack[step_w, t, :, lanes] = jnp.where(keep, moved, 0.0).astype(plain.dtype)
        return carry

    lax.fori_loop(0, frames * (rows + 2 * REACH), shift_row, 0)

    def advance(step, first, last):
        for h in range(first, last):
            for way in range(2):

                @pl.when(receives(way, step))
                def _():
                    arrival(way, step, h).wait_recv()

                if step + 1 < col_count - 1:

                    @pl.when(sends(way, step + 1))
                    def _():
                        hop(way, step + 1, h).start()

    both = jnp.minimum(j, col_count - 1 - j)
    more_after = j < col_count - 1 - j

    def owner_of(slot):
        paired = j + ((slot + 1) // 2) * (1 if slot % 2 == 0 else -1)
        single = jnp.where(more_after, j + (slot - both), j - (slot - both))
        return jnp.where(slot <= 2 * both, paired, single)

    group = block // col_count
    scale = 1.0 / (frames * rows * ha_count * width)
    lane_block = lax.broadcasted_iota(jnp.int32, (group, channels), 1) // block

    def compute(slot, first, last):
        depth = (last - first) * width
        owner = owner_of(slot)

        def products(step_h, carry):
            start = pl.multiple_of((STEPS - 1 - step_h + first) * width, width)
            own = stack[:, :, :, pl.ds(start, depth)].reshape(STEPS * frames * block, depth)
            field = jnp.concatenate(
                [others[h, owner].reshape(frames * block, width) for h in range(first, last)], axis=1
            )
            result = lax.dot_general(
                own, field, (((1,), (1,)), ((), ())), preferred_element_type=jnp.float32
            )
            if last < rows:
                early[step_h] = result
                return carry
            if first > 0:
                result = result + early[step_h]
            spare = jnp.zeros((result.shape[0], channels - result.shape[1]), jnp.float32)
            result = jnp.concatenate([result * scale, spare], axis=1)
            moved = [result] + [pltpu.roll(result, k * block, axis=1) for k in range(1, col_count)]
            for step_w in range(STEPS):
                for step_t in range(STEPS):
                    shift = step_t - REACH
                    packed = jnp.zeros((group, channels), jnp.float32)
                    for g in range(col_count):
                        total = None
                        for t in range(frames):
                            if 0 <= t + shift < frames:
                                row = (step_w * frames + t) * block + g * group
                                term = moved[(g - t - shift) % col_count][row : row + group]
                                total = term if total is None else total + term
                        if total is not None:
                            packed = jnp.where(lane_block == g, total, packed)
                    part[slot, step_t * STEPS * STEPS + step_h * STEPS + step_w] = packed
            return carry

        lax.fori_loop(0, STEPS, products, 0)

    near_copies, far_copies = {}, {}

    turns = [*range(1, half), 0]

    def pass_near(slot):
        for r in turns:
            target = lax.rem(place + r, half)
            near_copies[slot, r] = pltpu.make_async_remote_copy(
                src_ref=part.at[slot, pl.ds(first_lag(2 * target + 1 - parity), span)],
                dst_ref=near.at[slot, r],
                send_sem=near_send.at[slot, r],
                recv_sem=near_recv.at[slot, r],
                device_id={"ha": partner},
                device_id_type=MESH,
            )
            near_copies[slot, r].start()

    def pass_far(slot):
        for r in turns:
            target = lax.rem(place + r, half)
            near_copies[slot, r].wait_recv()
            mixed[slot, r] = part[slot, pl.ds(first_lag(2 * target + parity), span)] + near[slot, r]
            if r > 0:
                far_copies[slot, r] = pltpu.make_async_remote_copy(
                    src_ref=mixed.at[slot, r],
                    dst_ref=far.at[slot, r - 1],
                    send_sem=far_send.at[slot, r - 1],
                    recv_sem=far_recv.at[slot, r - 1],
                    device_id={"ha": 2 * target + parity},
                    device_id_type=MESH,
                )
                far_copies[slot, r].start()

    middle = rows // 2
    for slot in range(col_count):
        if slot == col_count - 1 and slot > 0 and middle > 0:
            advance(slot - 1, 0, middle)
            pass_far(slot - 1)
            compute(slot, 0, middle)
            advance(slot - 1, middle, rows)
            compute(slot, middle, rows)
        else:
            if slot > 0:
                advance(slot - 1, 0, rows)
                pass_far(slot - 1)
            compute(slot, 0, rows)
        pass_near(slot)
    pass_far(col_count - 1)

    for slot in range(col_count):
        for r in range(1, half):
            far_copies[slot, r].wait_recv()
        total = mixed[slot, 0]
        for r in range(1, half):
            total = total + far[slot, r - 1]
        summed[owner_of(slot)] = total

    for k in range(span):
        tiles = [summed[q, k] for q in range(col_count)]
        for g in range(col_count):
            rows_out = jnp.zeros((group, channels), jnp.float32)
            for q in range(col_count):
                turn = (q - g) * block % channels
                tile = pltpu.roll(tiles[q], turn, axis=1) if turn else tiles[q]
                rows_out = jnp.where(lane_block == q, tile, rows_out)
            out_ref[g * group : (g + 1) * group, k * channels : (k + 1) * channels] = rows_out

    for copy in list(far_copies.values()) + list(near_copies.values()):
        copy.wait_send()
    for step in range(col_count - 1):
        for way in range(2):

            @pl.when(sends(way, step))
            def _():
                for h in range(rows):
                    hop(way, step, h).wait_send()

    for way, has in ((0, has_after), (1, has_before)):

        @pl.when(has)
        def _():
            for r in range(REACH):
                halo(way, r).wait_send()


def body(ha_count, col_count, features):
    frames, rows, block, width = features.shape
    channels = block * col_count
    lag_count = STEPS**3
    share, span = window_plan(lag_count, channels, ha_count)
    half = ha_count // 2
    group = block // col_count
    dma = pltpu.SemaphoreType.DMA
    lines = max(col_count - 1, 1)
    window = pl.pallas_call(
        functools.partial(kernel, ha_count, col_count),
        out_shape=jax.ShapeDtypeStruct((block, span * channels), jnp.float32),
        in_specs=[pl.BlockSpec(memory_space=pl.ANY)],
        out_specs=pl.BlockSpec(memory_space=pltpu.VMEM),
        scratch_shapes=[
            pltpu.VMEM((frames, block, (rows + 2 * REACH) * width), features.dtype),
            pltpu.VMEM((STEPS, frames, block, (rows + 2 * REACH) * width), features.dtype),
            pltpu.VMEM((rows, col_count, frames, block, width), features.dtype),
            pltpu.VMEM((col_count, lag_count, group, channels), jnp.float32),
            pltpu.VMEM((col_count, half, span, group, channels), jnp.float32),
            pltpu.VMEM((col_count, half, span, group, channels), jnp.float32),
            pltpu.VMEM((col_count, half, span, group, channels), jnp.float32),
            pltpu.VMEM((col_count, span, group, channels), jnp.float32),
            pltpu.VMEM((STEPS, STEPS * frames * block, frames * block), jnp.float32),
            dma((2, rows)),
            dma((2, REACH)),
            dma((2, REACH)),
            dma((2, lines, rows)),
            dma((2, lines, rows)),
            dma((col_count, half)),
            dma((col_count, half)),
            dma((col_count, half)),
            dma((col_count, half)),
        ],
        compiler_params=pltpu.CompilerParams(collective_id=0, has_side_effects=True),
        name="lag_cov",
    )(features)
    i = lax.axis_index("ha")
    first = jnp.minimum(i * share // channels, lag_count - span)
    return lax.dynamic_slice_in_dim(window, i * share - first * channels, share, 1)


def solution(mesh):
    in_specs = (P(None, "ha", "col", None),)
    out_specs = P("col", "ha")
    counts = (mesh.shape["ha"], mesh.shape["col"])
    return jax.shard_map(
        functools.partial(body, *counts), mesh=mesh, in_specs=in_specs, out_specs=out_specs, check_vma=False
    )
```

```python
import functools

import jax
import jax.numpy as jnp
from jax import lax
from jax.experimental import pallas as pl
from jax.experimental.pallas import tpu as pltpu
from jax.sharding import PartitionSpec as P

MESH = pl.DeviceIdType.MESH
REACH = 2
STEPS = 2 * REACH + 1


def window_plan(lag_count, channels, ha_count):
    share = lag_count * channels // ha_count
    spans = [-(-(i + 1) * share // channels) - i * share // channels for i in range(ha_count)]
    return share, max(spans)


def kernel(
    ha_count, col_count, x_ref, out_ref, base, stack, others, part, near, mixed, far, summed, early,
    local_sem, halo_send, halo_recv, line_send, line_recv, near_send, near_recv, far_send, far_recv,
):
    frames, rows, block, width = x_ref.shape
    channels = block * col_count
    lag_count = STEPS**3
    share, span = window_plan(lag_count, channels, ha_count)
    i, j = lax.axis_index("ha"), lax.axis_index("col")
    half = ha_count // 2
    parity, place = lax.rem(i, 2), lax.div(i, 2)
    partner = i + 1 - 2 * parity

    def first_lag(index):
        return jnp.minimum(lax.div(index * share, channels), lag_count - span)

    barrier = pltpu.get_barrier_semaphore()
    for step in range(1, ha_count):
        pl.semaphore_signal(
            barrier, inc=1, device_id={"ha": lax.rem(i + step, ha_count)}, device_id_type=MESH
        )

    @pl.when(j > 0)
    def _():
        pl.semaphore_signal(barrier, inc=1, device_id={"col": j - 1}, device_id_type=MESH)

    @pl.when(j < col_count - 1)
    def _():
        pl.semaphore_signal(barrier, inc=1, device_id={"col": j + 1}, device_id_type=MESH)

    own_copies = []
    for h in range(rows):
        own_copies.append(
            pltpu.make_async_copy(
                x_ref.at[:, h], others.at[h, j], local_sem.at[0, h]
            )
        )
        own_copies.append(
            pltpu.make_async_copy(
                x_ref.at[:, h], base.at[:, :, pl.ds((h + REACH) * width, width)], local_sem.at[1, h]
            )
        )
    for copy in own_copies:
        copy.start()

    ends = (j > 0).astype(jnp.int32) + (j < col_count - 1).astype(jnp.int32)
    pl.semaphore_wait(barrier, ha_count - 1 + ends)

    def halo(way, r):
        source = rows - REACH + r if way == 0 else r
        slot = r if way == 0 else rows + REACH + r
        return pltpu.make_async_remote_copy(
            src_ref=x_ref.at[:, source],
            dst_ref=base.at[:, :, pl.ds(slot * width, width)],
            send_sem=halo_send.at[way, r],
            recv_sem=halo_recv.at[way, r],
            device_id={"ha": (i + 1) if way == 0 else (i - 1)},
            device_id_type=MESH,
        )

    def hop(way, step, h):
        sign = 1 if way == 0 else -1
        owner = j - sign * step
        return pltpu.make_async_remote_copy(
            src_ref=x_ref.at[:, h] if step == 0 else others.at[h, owner],
            dst_ref=others.at[h, owner],
            send_sem=line_send.at[way, step, h],
            recv_sem=line_recv.at[way, step, h],
            device_id={"col": j + sign},
            device_id_type=MESH,
        )

    def sends(way, step):
        if way == 0:
            return jnp.logical_and(j < col_count - 1, j - step >= 0)
        return jnp.logical_and(j > 0, j + step <= col_count - 1)

    def receives(way, step):
        return j - 1 - step >= 0 if way == 0 else j + 1 + step <= col_count - 1

    def arrival(way, step, h):
        sign = 1 if way == 0 else -1
        owner = j - sign * (step + 1)
        return pltpu.make_async_remote_copy(
            src_ref=others.at[h, owner],
            dst_ref=others.at[h, owner],
            send_sem=line_send.at[way, step, h],
            recv_sem=line_recv.at[way, step, h],
            device_id={"col": j - sign},
            device_id_type=MESH,
        )

    for way in range(2):

        @pl.when(sends(way, 0))
        def _():
            for h in range(rows):
                hop(way, 0, h).start()

    has_after, has_before = i < ha_count - 1, i > 0
    for way, has in ((0, has_after), (1, has_before)):

        @pl.when(has)
        def _():
            for r in range(REACH):
                halo(way, r).start()

    for copy in own_copies:
        copy.wait()

    @pl.when(jnp.logical_not(has_before))
    def _():
        base[:, :, : REACH * width] = jnp.zeros((frames, block, REACH * width), base.dtype)

    @pl.when(jnp.logical_not(has_after))
    def _():
        base[:, :, (rows + REACH) * width :] = jnp.zeros((frames, block, REACH * width), base.dtype)

    for way, has_in in ((0, has_before), (1, has_after)):

        @pl.when(has_in)
        def _():
            for r in range(REACH):
                halo(way, r).wait_recv()

    column = lax.broadcasted_iota(jnp.int32, (block, width), 1)

    def shift_row(index, carry):
        t, h = lax.div(index, rows + 2 * REACH), lax.rem(index, rows + 2 * REACH)
        lanes = pl.ds(pl.multiple_of(h * width, width), width)
        plain = base[t, :, lanes]
        wide = plain.astype(jnp.float32)
        for step_w in range(STEPS):
            shift = step_w - REACH
            if shift == 0:
                stack[step_w, t, :, lanes] = plain
            else:
                moved = pltpu.roll(wide, shift % width, axis=1)
                keep = column >= shift if shift > 0 else column < width + shift
                stack[step_w, t, :, lanes] = jnp.where(keep, moved, 0.0).astype(plain.dtype)
        return carry

    lax.fori_loop(0, frames * (rows + 2 * REACH), shift_row, 0)

    def advance(step, first, last):
        for h in range(first, last):
            for way in range(2):

                @pl.when(receives(way, step))
                def _():
                    arrival(way, step, h).wait_recv()

                if step + 1 < col_count - 1:

                    @pl.when(sends(way, step + 1))
                    def _():
                        hop(way, step + 1, h).start()

    both = jnp.minimum(j, col_count - 1 - j)
    more_after = j < col_count - 1 - j

    def owner_of(slot):
        paired = j + ((slot + 1) // 2) * (1 if slot % 2 == 0 else -1)
        single = jnp.where(more_after, j + (slot - both), j - (slot - both))
        return jnp.where(slot <= 2 * both, paired, single)

    group = block // col_count
    scale = 1.0 / (frames * rows * ha_count * width)
    lane_block = lax.broadcasted_iota(jnp.int32, (group, channels), 1) // block

    def compute(slot, first, last):
        depth = (last - first) * width
        owner = owner_of(slot)

        def products(step_h, carry):
            start = pl.multiple_of((STEPS - 1 - step_h + first) * width, width)
            own = stack[:, :, :, pl.ds(start, depth)].reshape(STEPS * frames * block, depth)
            field = jnp.concatenate(
                [others[h, owner].reshape(frames * block, width) for h in range(first, last)], axis=1
            )
            result = lax.dot_general(
                own, field, (((1,), (1,)), ((), ())), preferred_element_type=jnp.float32
            )
            if first > 0:
                result = result + early[step_h]
            if last < rows:
                early[step_h] = result
                return carry
            spare = jnp.zeros((result.shape[0], channels - result.shape[1]), jnp.float32)
            result = jnp.concatenate([result * scale, spare], axis=1)
            moved = [result] + [pltpu.roll(result, k * block, axis=1) for k in range(1, col_count)]
            for step_w in range(STEPS):
                for step_t in range(STEPS):
                    shift = step_t - REACH
                    packed = jnp.zeros((group, channels), jnp.float32)
                    for g in range(col_count):
                        total = None
                        for t in range(frames):
                            if 0 <= t + shift < frames:
                                row = (step_w * frames + t) * block + g * group
                                term = moved[(g - t - shift) % col_count][row : row + group]
                                total = term if total is None else total + term
                        if total is not None:
                            packed = jnp.where(lane_block == g, total, packed)
                    part[slot, step_t * STEPS * STEPS + step_h * STEPS + step_w] = packed
            return carry

        lax.fori_loop(0, STEPS, products, 0)

    near_copies, far_copies = {}, {}

    turns = [*range(1, half), 0]

    def pass_near(slot):
        for r in turns:
            target = lax.rem(place + r, half)
            near_copies[slot, r] = pltpu.make_async_remote_copy(
                src_ref=part.at[slot, pl.ds(first_lag(2 * target + 1 - parity), span)],
                dst_ref=near.at[slot, r],
                send_sem=near_send.at[slot, r],
                recv_sem=near_recv.at[slot, r],
                device_id={"ha": partner},
                device_id_type=MESH,
            )
            near_copies[slot, r].start()

    def pass_far(slot):
        for r in turns:
            target = lax.rem(place + r, half)
            near_copies[slot, r].wait_recv()
            mixed[slot, r] = part[slot, pl.ds(first_lag(2 * target + parity), span)] + near[slot, r]
            if r > 0:
                far_copies[slot, r] = pltpu.make_async_remote_copy(
                    src_ref=mixed.at[slot, r],
                    dst_ref=far.at[slot, r - 1],
                    send_sem=far_send.at[slot, r - 1],
                    recv_sem=far_recv.at[slot, r - 1],
                    device_id={"ha": 2 * target + parity},
                    device_id_type=MESH,
                )
                far_copies[slot, r].start()

    cuts = sorted({0, rows // 2, rows - 1, rows})
    if col_count > 1:
        advance(0, 0, rows)
    for slot in range(col_count):
        if slot < 2:
            compute(slot, 0, rows)
            if slot > 0:
                pass_far(slot - 1)
        elif slot < col_count - 1:
            advance(slot - 1, 0, rows)
            pass_far(slot - 1)
            compute(slot, 0, rows)
        else:
            for first, last in zip(cuts, cuts[1:]):
                advance(slot - 1, first, last)
                if first == 0:
                    pass_far(slot - 1)
                compute(slot, first, last)
        pass_near(slot)
    pass_far(col_count - 1)

    for slot in range(col_count):
        for r in range(1, half):
            far_copies[slot, r].wait_recv()
        total = mixed[slot, 0]
        for r in range(1, half):
            total = total + far[slot, r - 1]
        summed[owner_of(slot)] = total

    for k in range(span):
        tiles = [summed[q, k] for q in range(col_count)]
        for g in range(col_count):
            rows_out = jnp.zeros((group, channels), jnp.float32)
            for q in range(col_count):
                turn = (q - g) * block % channels
                tile = pltpu.roll(tiles[q], turn, axis=1) if turn else tiles[q]
                rows_out = jnp.where(lane_block == q, tile, rows_out)
            out_ref[g * group : (g + 1) * group, k * channels : (k + 1) * channels] = rows_out

    for copy in list(far_copies.values()) + list(near_copies.values()):
        copy.wait_send()
    for step in range(col_count - 1):
        for way in range(2):

            @pl.when(sends(way, step))
            def _():
                for h in range(rows):
                    hop(way, step, h).wait_send()

    for way, has in ((0, has_after), (1, has_before)):

        @pl.when(has)
        def _():
            for r in range(REACH):
                halo(way, r).wait_send()


def body(ha_count, col_count, features):
    frames, rows, block, width = features.shape
    channels = block * col_count
    lag_count = STEPS**3
    share, span = window_plan(lag_count, channels, ha_count)
    half = ha_count // 2
    group = block // col_count
    dma = pltpu.SemaphoreType.DMA
    lines = max(col_count - 1, 1)
    window = pl.pallas_call(
        functools.partial(kernel, ha_count, col_count),
        out_shape=jax.ShapeDtypeStruct((block, span * channels), jnp.float32),
        in_specs=[pl.BlockSpec(memory_space=pl.ANY)],
        out_specs=pl.BlockSpec(memory_space=pltpu.VMEM),
        scratch_shapes=[
            pltpu.VMEM((frames, block, (rows + 2 * REACH) * width), features.dtype),
            pltpu.VMEM((STEPS, frames, block, (rows + 2 * REACH) * width), features.dtype),
            pltpu.VMEM((rows, col_count, frames, block, width), features.dtype),
            pltpu.VMEM((col_count, lag_count, group, channels), jnp.float32),
            pltpu.VMEM((col_count, half, span, group, channels), jnp.float32),
            pltpu.VMEM((col_count, half, span, group, channels), jnp.float32),
            pltpu.VMEM((col_count, half, span, group, channels), jnp.float32),
            pltpu.VMEM((col_count, span, group, channels), jnp.float32),
            pltpu.VMEM((STEPS, STEPS * frames * block, frames * block), jnp.float32),
            dma((2, rows)),
            dma((2, REACH)),
            dma((2, REACH)),
            dma((2, lines, rows)),
            dma((2, lines, rows)),
            dma((col_count, half)),
            dma((col_count, half)),
            dma((col_count, half)),
            dma((col_count, half)),
        ],
        compiler_params=pltpu.CompilerParams(collective_id=0, has_side_effects=True),
        name="lag_cov",
    )(features)
    i = lax.axis_index("ha")
    first = jnp.minimum(i * share // channels, lag_count - span)
    return lax.dynamic_slice_in_dim(window, i * share - first * channels, share, 1)


def solution(mesh):
    in_specs = (P(None, "ha", "col", None),)
    out_specs = P("col", "ha")
    counts = (mesh.shape["ha"], mesh.shape["col"])
    return jax.shard_map(
        functools.partial(body, *counts), mesh=mesh, in_specs=in_specs, out_specs=out_specs, check_vma=False
    )
```

```python
import functools

import jax
import jax.numpy as jnp
from jax import lax
from jax.experimental import pallas as pl
from jax.experimental.pallas import tpu as pltpu
from jax.sharding import PartitionSpec as P

MESH = pl.DeviceIdType.MESH
REACH = 2
STEPS = 2 * REACH + 1


def window_plan(lag_count, channels, ha_count):
    share = lag_count * channels // ha_count
    spans = [-(-(i + 1) * share // channels) - i * share // channels for i in range(ha_count)]
    return share, max(spans)


def kernel(
    ha_count, col_count, x_ref, out_ref, base, stack, others, part, near, mixed, far, summed, early,
    local_sem, halo_send, halo_recv, line_send, line_recv, near_send, near_recv, far_send, far_recv,
):
    frames, rows, block, width = x_ref.shape
    channels = block * col_count
    lag_count = STEPS**3
    share, span = window_plan(lag_count, channels, ha_count)
    i, j = lax.axis_index("ha"), lax.axis_index("col")
    half = ha_count // 2
    parity, place = lax.rem(i, 2), lax.div(i, 2)
    partner = i + 1 - 2 * parity

    def first_lag(index):
        return jnp.minimum(lax.div(index * share, channels), lag_count - span)

    barrier = pltpu.get_barrier_semaphore()
    for step in range(1, ha_count):
        pl.semaphore_signal(
            barrier, inc=1, device_id={"ha": lax.rem(i + step, ha_count)}, device_id_type=MESH
        )

    @pl.when(j > 0)
    def _():
        pl.semaphore_signal(barrier, inc=1, device_id={"col": j - 1}, device_id_type=MESH)

    @pl.when(j < col_count - 1)
    def _():
        pl.semaphore_signal(barrier, inc=1, device_id={"col": j + 1}, device_id_type=MESH)

    own_copies = []
    for h in range(rows):
        own_copies.append(
            pltpu.make_async_copy(
                x_ref.at[:, h], others.at[h, j], local_sem.at[0, h]
            )
        )
        own_copies.append(
            pltpu.make_async_copy(
                x_ref.at[:, h], base.at[:, :, pl.ds((h + REACH) * width, width)], local_sem.at[1, h]
            )
        )
    for copy in own_copies:
        copy.start()

    ends = (j > 0).astype(jnp.int32) + (j < col_count - 1).astype(jnp.int32)
    pl.semaphore_wait(barrier, ha_count - 1 + ends)

    def halo(way, r):
        source = rows - REACH + r if way == 0 else r
        slot = r if way == 0 else rows + REACH + r
        return pltpu.make_async_remote_copy(
            src_ref=x_ref.at[:, source],
            dst_ref=base.at[:, :, pl.ds(slot * width, width)],
            send_sem=halo_send.at[way, r],
            recv_sem=halo_recv.at[way, r],
            device_id={"ha": (i + 1) if way == 0 else (i - 1)},
            device_id_type=MESH,
        )

    def hop(way, step, h):
        sign = 1 if way == 0 else -1
        owner = j - sign * step
        return pltpu.make_async_remote_copy(
            src_ref=x_ref.at[:, h] if step == 0 else others.at[h, owner],
            dst_ref=others.at[h, owner],
            send_sem=line_send.at[way, step, h],
            recv_sem=line_recv.at[way, step, h],
            device_id={"col": j + sign},
            device_id_type=MESH,
        )

    def sends(way, step):
        if way == 0:
            return jnp.logical_and(j < col_count - 1, j - step >= 0)
        return jnp.logical_and(j > 0, j + step <= col_count - 1)

    def receives(way, step):
        return j - 1 - step >= 0 if way == 0 else j + 1 + step <= col_count - 1

    def arrival(way, step, h):
        sign = 1 if way == 0 else -1
        owner = j - sign * (step + 1)
        return pltpu.make_async_remote_copy(
            src_ref=others.at[h, owner],
            dst_ref=others.at[h, owner],
            send_sem=line_send.at[way, step, h],
            recv_sem=line_recv.at[way, step, h],
            device_id={"col": j - sign},
            device_id_type=MESH,
        )

    has_after, has_before = i < ha_count - 1, i > 0
    for way, has in ((0, has_after), (1, has_before)):

        @pl.when(has)
        def _():
            for r in range(REACH):
                halo(way, r).start()

    for way in range(2):

        @pl.when(sends(way, 0))
        def _():
            for h in range(rows):
                hop(way, 0, h).start()

    for copy in own_copies:
        copy.wait()

    @pl.when(jnp.logical_not(has_before))
    def _():
        base[:, :, : REACH * width] = jnp.zeros((frames, block, REACH * width), base.dtype)

    @pl.when(jnp.logical_not(has_after))
    def _():
        base[:, :, (rows + REACH) * width :] = jnp.zeros((frames, block, REACH * width), base.dtype)

    for way, has_in in ((0, has_before), (1, has_after)):

        @pl.when(has_in)
        def _():
            for r in range(REACH):
                halo(way, r).wait_recv()

    column = lax.broadcasted_iota(jnp.int32, (block, width), 1)

    def shift_row(index, carry):
        t, h = lax.div(index, rows + 2 * REACH), lax.rem(index, rows + 2 * REACH)
        lanes = pl.ds(pl.multiple_of(h * width, width), width)
        plain = base[t, :, lanes]
        wide = plain.astype(jnp.float32)
        for step_w in range(STEPS):
            shift = step_w - REACH
            if shift == 0:
                stack[step_w, t, :, lanes] = plain
            else:
                moved = pltpu.roll(wide, shift % width, axis=1)
                keep = column >= shift if shift > 0 else column < width + shift
                stack[step_w, t, :, lanes] = jnp.where(keep, moved, 0.0).astype(plain.dtype)
        return carry

    lax.fori_loop(0, frames * (rows + 2 * REACH), shift_row, 0)

    def advance(step, first, last):
        for h in range(first, last):
            for way in range(2):

                @pl.when(receives(way, step))
                def _():
                    arrival(way, step, h).wait_recv()

                if step + 1 < col_count - 1:

                    @pl.when(sends(way, step + 1))
                    def _():
                        hop(way, step + 1, h).start()

    both = jnp.minimum(j, col_count - 1 - j)
    more_after = j < col_count - 1 - j

    def owner_of(slot):
        paired = j + ((slot + 1) // 2) * (1 if slot % 2 == 0 else -1)
        single = jnp.where(more_after, j + (slot - both), j - (slot - both))
        return jnp.where(slot <= 2 * both, paired, single)

    group = block // col_count
    scale = 1.0 / (frames * rows * ha_count * width)
    lane_block = lax.broadcasted_iota(jnp.int32, (group, channels), 1) // block

    def compute(slot, first, last):
        depth = (last - first) * width
        owner = owner_of(slot)

        def products(step_h, carry):
            start = pl.multiple_of((STEPS - 1 - step_h + first) * width, width)
            own = stack[:, :, :, pl.ds(start, depth)].reshape(STEPS * frames * block, depth)
            field = jnp.concatenate(
                [others[h, owner].reshape(frames * block, width) for h in range(first, last)], axis=1
            )
            result = lax.dot_general(
                own, field, (((1,), (1,)), ((), ())), preferred_element_type=jnp.float32
            )
            if first > 0:
                result = result + early[step_h]
            if last < rows:
                early[step_h] = result
                return carry
            spare = jnp.zeros((result.shape[0], channels - result.shape[1]), jnp.float32)
            result = jnp.concatenate([result * scale, spare], axis=1)
            moved = [result] + [pltpu.roll(result, k * block, axis=1) for k in range(1, col_count)]
            for step_w in range(STEPS):
                for step_t in range(STEPS):
                    shift = step_t - REACH
                    packed = jnp.zeros((group, channels), jnp.float32)
                    for g in range(col_count):
                        total = None
                        for t in range(frames):
                            if 0 <= t + shift < frames:
                                row = (step_w * frames + t) * block + g * group
                                term = moved[(g - t - shift) % col_count][row : row + group]
                                total = term if total is None else total + term
                        if total is not None:
                            packed = jnp.where(lane_block == g, total, packed)
                    part[slot, step_t * STEPS * STEPS + step_h * STEPS + step_w] = packed
            return carry

        lax.fori_loop(0, STEPS, products, 0)

    near_copies, far_copies = {}, {}

    turns = [*range(1, half), 0]

    def pass_near(slot):
        for r in turns:
            target = lax.rem(place + r, half)
            near_copies[slot, r] = pltpu.make_async_remote_copy(
                src_ref=part.at[slot, pl.ds(first_lag(2 * target + 1 - parity), span)],
                dst_ref=near.at[slot, r],
                send_sem=near_send.at[slot, r],
                recv_sem=near_recv.at[slot, r],
                device_id={"ha": partner},
                device_id_type=MESH,
            )
            near_copies[slot, r].start()

    def pass_far(slot):
        for r in turns:
            target = lax.rem(place + r, half)
            near_copies[slot, r].wait_recv()
            mixed[slot, r] = part[slot, pl.ds(first_lag(2 * target + parity), span)] + near[slot, r]
            if r > 0:
                far_copies[slot, r] = pltpu.make_async_remote_copy(
                    src_ref=mixed.at[slot, r],
                    dst_ref=far.at[slot, r - 1],
                    send_sem=far_send.at[slot, r - 1],
                    recv_sem=far_recv.at[slot, r - 1],
                    device_id={"ha": 2 * target + parity},
                    device_id_type=MESH,
                )
                far_copies[slot, r].start()

    cuts = sorted({0, rows // 2, rows - 1, rows})
    if col_count > 1:
        advance(0, 0, rows)
    for slot in range(col_count):
        if slot < 2:
            compute(slot, 0, rows)
            if slot > 0:
                pass_far(slot - 1)
        elif slot < col_count - 1:
            advance(slot - 1, 0, rows)
            pass_far(slot - 1)
            compute(slot, 0, rows)
        else:
            for first, last in zip(cuts, cuts[1:]):
                advance(slot - 1, first, last)
                if first == 0:
                    pass_far(slot - 1)
                compute(slot, first, last)
        pass_near(slot)
    pass_far(col_count - 1)

    for slot in range(col_count):
        for r in range(1, half):
            far_copies[slot, r].wait_recv()
        total = mixed[slot, 0]
        for r in range(1, half):
            total = total + far[slot, r - 1]
        summed[owner_of(slot)] = total

    for k in range(span):
        tiles = [summed[q, k] for q in range(col_count)]
        for g in range(col_count):
            rows_out = jnp.zeros((group, channels), jnp.float32)
            for q in range(col_count):
                turn = (q - g) * block % channels
                tile = pltpu.roll(tiles[q], turn, axis=1) if turn else tiles[q]
                rows_out = jnp.where(lane_block == q, tile, rows_out)
            out_ref[g * group : (g + 1) * group, k * channels : (k + 1) * channels] = rows_out

    for copy in list(far_copies.values()) + list(near_copies.values()):
        copy.wait_send()
    for step in range(col_count - 1):
        for way in range(2):

            @pl.when(sends(way, step))
            def _():
                for h in range(rows):
                    hop(way, step, h).wait_send()

    for way, has in ((0, has_after), (1, has_before)):

        @pl.when(has)
        def _():
            for r in range(REACH):
                halo(way, r).wait_send()


def body(ha_count, col_count, features):
    frames, rows, block, width = features.shape
    channels = block * col_count
    lag_count = STEPS**3
    share, span = window_plan(lag_count, channels, ha_count)
    half = ha_count // 2
    group = block // col_count
    dma = pltpu.SemaphoreType.DMA
    lines = max(col_count - 1, 1)
    window = pl.pallas_call(
        functools.partial(kernel, ha_count, col_count),
        out_shape=jax.ShapeDtypeStruct((block, span * channels), jnp.float32),
        in_specs=[pl.BlockSpec(memory_space=pl.ANY)],
        out_specs=pl.BlockSpec(memory_space=pltpu.VMEM),
        scratch_shapes=[
            pltpu.VMEM((frames, block, (rows + 2 * REACH) * width), features.dtype),
            pltpu.VMEM((STEPS, frames, block, (rows + 2 * REACH) * width), features.dtype),
            pltpu.VMEM((rows, col_count, frames, block, width), features.dtype),
            pltpu.VMEM((col_count, lag_count, group, channels), jnp.float32),
            pltpu.VMEM((col_count, half, span, group, channels), jnp.float32),
            pltpu.VMEM((col_count, half, span, group, channels), jnp.float32),
            pltpu.VMEM((col_count, half, span, group, channels), jnp.float32),
            pltpu.VMEM((col_count, span, group, channels), jnp.float32),
            pltpu.VMEM((STEPS, STEPS * frames * block, frames * block), jnp.float32),
            dma((2, rows)),
            dma((2, REACH)),
            dma((2, REACH)),
            dma((2, lines, rows)),
            dma((2, lines, rows)),
            dma((col_count, half)),
            dma((col_count, half)),
            dma((col_count, half)),
            dma((col_count, half)),
        ],
        compiler_params=pltpu.CompilerParams(collective_id=0, has_side_effects=True),
        name="lag_cov",
    )(features)
    i = lax.axis_index("ha")
    first = jnp.minimum(i * share // channels, lag_count - span)
    return lax.dynamic_slice_in_dim(window, i * share - first * channels, share, 1)


def solution(mesh):
    in_specs = (P(None, "ha", "col", None),)
    out_specs = P("col", "ha")
    counts = (mesh.shape["ha"], mesh.shape["col"])
    return jax.shard_map(
        functools.partial(body, *counts), mesh=mesh, in_specs=in_specs, out_specs=out_specs, check_vma=False
    )
```
